32 devices in a mesh: row: 4 (over y, x), col: 8 (over z, core).
Axes of the slice: x: 2, y: 2, z: 4, core: 2. Of those that a mesh axis runs over, the one named last changes fastest.
Arguments:
- tokens: bfloat16 [512, 7168], P('col', 'row'), may hold values from -6 to 6
- routes: int32 [512, 8], P('col'), may hold values from 0 to 15, all different within a row; in each aligned block of 64 rows (0 to 63, 64 to 127, ...) at most 40 rows name the same one
- gates: float32 [512, 8], P('col'), may hold values from 0.05 to 0.5
- w_gate: bfloat16 [16, 7168, 2048], P('col', None, 'row'), may hold values from -0.0625 to 0.0625
- w_up: bfloat16 [16, 7168, 2048], P('col', None, 'row'), may hold values from -0.0625 to 0.0625
- w_down: bfloat16 [16, 2048, 7168], P('col', 'row'), may hold values from -0.125 to 0.125
Outputs:
- mixed: bfloat16 [512, 7168], P('col', 'row')
The draws below stay inside these ranges and needn't reach their ends.
Inputs may be any that keep to these rules, and one draw needn't show every extreme that they name: `routes`: the 8 experts of a token are distinct. Among the 64 tokens of one index of col (aligned blocks of 64 tokens), no expert is chosen more than 40 times, and some expert is chosen exactly 40 times.
All inputs are finite; a program needn't handle non-finite values.
Results may differ from the reference program's by a relative error of at most 0.015.
Values may be sent and summed in bfloat16 or wider, within the bound.
A program may use at most 128 MiB of HBM per device.

```python
import math
import jax
import jax.numpy as jnp
import numpy as np
from jax import lax

D = 7168
FF = 2048
TOP = 8
TOK_DEV = 64
CAP = 40
EXPERTS = 16
TOKENS = 512
SLOTS = 320
FF_BLOCK = 512
N_ROW = 4
N_COL = 8


def steps_of(rng, shape, cuts, least, high):
    def one(dim, parts):
        steps = jax.random.uniform(jax.random.fold_in(jax.random.fold_in(rng, 6), dim), (parts,), jnp.float32, least / len(cuts), high / len(cuts))
        return jnp.repeat(jnp.exp(steps), shape[dim] // parts).reshape((-1,) + (1,) * (len(shape) - dim - 1))

    factor_of = one(*cuts[0])
    for cut in cuts[1:]:
        factor_of = factor_of * one(*cut)
    return factor_of


def deal_out(rng, own, number, rows, count, top, most, lean):
    sequence = jax.random.permutation(rng, count)
    packed, usual = portions_of(count, rows * top, most, lean, True), portions_of(count, rows * top, most, lean, False)
    places = jnp.arange(count)

    def named(lengths, turn):
        used = int((lengths > 0).sum())
        fixed = max(1, used // 4)
        moved = fixed + (places - fixed + turn * (used - fixed)) % max(1, count - fixed)
        return jnp.zeros((count,), jnp.int32).at[sequence[jnp.where(places < fixed, places, moved)]].set(jnp.asarray(lengths, jnp.int32))

    lengths = jnp.where(number % 4 == 0, named(packed, number // 4), named(usual, number - number // 4 - 1))
    mixed = jax.random.permutation(jax.random.fold_in(own, 3), count)
    donor, taker = mixed[0:count // 2 * 2:2], mixed[1:count // 2 * 2:2]
    margin = jnp.minimum(lengths[donor] - 1, most - lengths[taker]) // 2
    margin = jnp.where((donor == sequence[0]) | (taker == sequence[0]) | (lengths[taker] == 0), 0, jnp.maximum(margin, 0))
    moved = jax.random.randint(jax.random.fold_in(own, 4), (count // 2,), 0, 1 << 20) % (margin + 1)
    lengths = lengths.at[donor].add(-moved).at[taker].add(moved)
    members = jnp.searchsorted(jnp.cumsum(lengths), jnp.arange(rows * top), side="right").astype(jnp.int32)
    grid = members.reshape(top, rows).T
    grid = grid[jax.random.permutation(jax.random.fold_in(own, 1), rows)]
    turn = jax.random.randint(jax.random.fold_in(own, 2), (rows, 1), 0, top)
    return jnp.take_along_axis(grid, (jnp.arange(top)[None, :] + turn) % top, axis=1)


def portions_of(count, total, most, lean, full):
    portions = [(1 << 20) // math.isqrt(standing ** lean) + 1 for standing in range(1, count + 1)]
    largest = most if full else min(most, max(-(-total // count), total * portions[0] // sum(portions)))
    least = 1 if total - largest >= count - 1 else 0
    given, surplus = [largest] + [least] * (count - 1), total - largest - least * (count - 1)
    while surplus > 0:
        movable = [i for i in range(1, count) if given[i] < largest] or [i for i in range(1, count) if given[i] < most]
        whole, left = sum([portions[i] for i in movable]), surplus
        for i in movable:
            extra = min(most - given[i], max(1, left * portions[i] // whole), surplus)
            given[i] = given[i] + extra
            surplus = surplus - extra
    return np.array(given)


def gaussian(key, shape, spread, limit, pieces=(), kind=jnp.bfloat16):
    factor_of = steps_of(key, shape, pieces, -0.22, 0.18) if pieces else 1.0
    result = jax.random.normal(key, shape, jnp.float32) * spread * factor_of
    return jnp.minimum(jnp.maximum(result, -limit), limit).astype(kind)


def setup_inputs(seed: int = 0) -> dict:
    key_list = jax.random.split(jax.random.key(seed), 7)
    tokens = gaussian(key_list[0], (TOKENS, D), 1.0, 6.0, ((0, 8), (1, 4)))
    routes_keys = jax.random.split(jax.random.fold_in(key_list[1], 1), TOKENS // TOK_DEV)
    routes_turns = jax.random.permutation(jax.random.fold_in(key_list[1], 3), TOKENS // TOK_DEV)
    routes = jax.vmap(lambda own, number: deal_out(jax.random.fold_in(key_list[1], 2), own, number, TOK_DEV, EXPERTS, TOP, CAP, 2))(routes_keys, routes_turns).reshape((TOKENS, TOP))
    gates = jnp.clip(0.05 + 0.45 * jax.random.uniform(key_list[2], (TOKENS, TOP), jnp.float32) ** steps_of(key_list[2], (TOKENS, TOP), ((0, 8),), -0.2, 0.2), 0.05, 0.5)
    w_gate = gaussian(key_list[3], (EXPERTS, D, FF), D ** -0.5, 0.0625, ((0, 8), (2, 4)))
    w_up = gaussian(key_list[4], (EXPERTS, D, FF), D ** -0.5, 0.0625, ((0, 8), (2, 4)))
    w_down = gaussian(key_list[5], (EXPERTS, FF, D), FF ** -0.5, 0.125, ((0, 8), (1, 4)))
    return dict(tokens=tokens, routes=routes, gates=gates, w_gate=w_gate, w_up=w_up, w_down=w_down)


def reference(tokens, routes, gates, w_gate, w_up, w_down):
    grouped = routes.reshape(N_COL, TOK_DEV * TOP)
    onehot = (grouped[:, :, None] == jnp.arange(EXPERTS, dtype=jnp.int32)[None, None, :]).astype(jnp.int32)
    before = jnp.cumsum(onehot, axis=1) - onehot
    position = jnp.sum(before * onehot, axis=2).astype(jnp.int32)
    group_ids = jnp.arange(N_COL, dtype=jnp.int32)[:, None]
    destination = (grouped * SLOTS + group_ids * CAP + position).reshape(-1)
    source_rows = jnp.arange(TOKENS * TOP, dtype=jnp.int32) // TOP
    dispatched = jnp.zeros((EXPERTS * SLOTS, D), jnp.bfloat16).at[destination].set(tokens[source_rows])
    dispatched = dispatched.reshape(EXPERTS, SLOTS, D)

    def expert(operands):
        inputs, gate_matrix, up_matrix, down_matrix = operands
        gate_act = jnp.dot(inputs, gate_matrix, preferred_element_type=jnp.float32)
        up_act = jnp.dot(inputs, up_matrix, preferred_element_type=jnp.float32)
        hidden = (jax.nn.silu(gate_act) * up_act).astype(jnp.bfloat16)
        partial_value = jnp.einsum("rcf,cfd->crd", hidden.reshape(SLOTS, N_ROW, FF_BLOCK).astype(jnp.float32),
                             down_matrix.reshape(N_ROW, FF_BLOCK, D).astype(jnp.float32))
        rounded = lax.optimization_barrier(partial_value.astype(jnp.bfloat16))
        return jnp.sum(rounded.astype(jnp.float32), axis=0).astype(jnp.bfloat16)

    outputs = lax.map(expert, (dispatched, w_gate, w_up, w_down))
    picked = outputs.reshape(EXPERTS * SLOTS, D)[destination].reshape(TOKENS, TOP, D)
    mixed = jnp.sum(gates[:, :, None] * picked.astype(jnp.float32), axis=1)
    return mixed.astype(jnp.bfloat16)
```

```python
import functools
import math

import jax
import jax.numpy as jnp
from jax import lax
from jax.experimental import pallas as pl
from jax.experimental.pallas import tpu as pltpu
from jax.sharding import PartitionSpec as P

MESH = pl.DeviceIdType.MESH
LANES = 128


def flip(value, mask):
    bit = 1
    while bit <= mask:
        if mask & bit:
            value = value + bit - 2 * bit * lax.rem(lax.div(value, bit), 2)
        bit *= 2
    return value


def kernel(
    side, depth, tokens, routes, gates, w_gate, w_up, w_down, out,
    x_all, g_all, w_buf, wd, acc, hid, part, pair, dx_in, dy_in, rx_in, ry_in, z_in,
    z_s, z_r, gz_s, gz_r, gp_s, gp_r, x_s, x_r, y_s, y_r, du_s, du_r, dl_s, dl_r,
    p_s, p_r, w_sem, wd_sem, own_sem,
    q_s, q_r, ou_s, ou_r, ol_s, ol_r, rx_s, rx_r, ry_s, ry_r, oz_s, oz_r,
):
    rows, feat = tokens.shape
    held, _, width = w_gate.shape
    half = rows // 2
    row, col = lax.axis_index("row"), lax.axis_index("col")
    yy, xx = lax.div(row, side), lax.rem(row, side)
    zz, core = lax.div(col, 2), lax.rem(col, 2)
    far = range(1, side)
    levels = range(depth)

    def row_of(dy, dx):
        return flip(yy, dy) * side + flip(xx, dx)

    def spot(j, plane=None):
        return (core if plane is None else plane) * depth + flip(zz, j)

    partner = (row, zz * 2 + 1 - core)

    def x_dev(dx):
        return (row_of(0, dx), col)

    def y_dev(dy):
        return (row_of(dy, 0), col)

    def z_dev(j):
        return (row, flip(zz, j) * 2 + core)

    sent = []

    def copy_of(src, dst, ss, rs, dev):
        return pltpu.make_async_remote_copy(
            src_ref=src, dst_ref=dst, send_sem=ss, recv_sem=rs,
            device_id=dev, device_id_type=MESH,
        )

    def send(src, dst, ss, rs, dev):
        copy = copy_of(src, dst, ss, rs, dev)
        copy.start()
        sent.append(copy)

    def arrive(ref, ss, rs):
        copy_of(ref, ref, ss, rs, partner).wait_recv()

    order = [(dy, dx) for dy in range(side) for dx in range(side)]
    per = 2 * held
    slots = w_buf.shape[0]
    units = len(order) * per

    def fetch(u):
        s, i = divmod(u, per)
        e, m = divmod(i, 2)
        start = pl.multiple_of(row_of(*order[s]) * feat, LANES)
        return pltpu.make_async_copy(
            (w_up if m else w_gate).at[e, pl.ds(start, feat), :],
            w_buf.at[u % slots],
            w_sem.at[u % slots],
        )

    for u in range(min(slots, units)):
        fetch(u).start()
    own = pltpu.make_async_copy(tokens, x_all.at[row, spot(0)], own_sem)
    own.start()

    lane = lax.broadcasted_iota(jnp.int32, (rows, LANES), 1)
    dense = jnp.zeros((rows, LANES), jnp.float32)
    for k in range(routes.shape[1]):
        dense = dense + jnp.where(lane == routes[:, k : k + 1], gates[:, k : k + 1], 0.0)
    g_all[spot(0)] = dense

    barrier = pltpu.get_barrier_semaphore()
    peers = [partner] + [x_dev(d) for d in far] + [y_dev(d) for d in far]
    peers += [z_dev(j) for j in levels[1:]]
    for peer in peers:
        pl.semaphore_signal(barrier, inc=1, device_id=peer, device_id_type=MESH)
    pl.semaphore_wait(barrier, len(peers))

    mine = x_all.at[row, spot(0)]
    for d in far:
        send(tokens, mine, x_s.at[d - 1, 0], x_r.at[d - 1, 0], x_dev(d))
        send(tokens, mine, y_s.at[d - 1, 0], y_r.at[d - 1, 0], y_dev(d))
    for j in levels[1:]:
        send(tokens, mine, z_s.at[j], z_r.at[j], z_dev(j))
    send(tokens, mine, p_s.at[0, 0, 0], p_r.at[0, 0, 0], partner)
    for j in levels[1:]:
        send(g_all.at[spot(0)], g_all.at[spot(0)], gz_s.at[j], gz_r.at[j], z_dev(j))
    send(g_all.at[spot(0)], g_all.at[spot(0)], gp_s.at[0], gp_r.at[0], partner)
    downs = [
        pltpu.make_async_copy(w_down.at[e], wd.at[pl.ds(e * width, width), :], wd_sem.at[e])
        for e in range(held)
    ]
    for down in downs:
        down.start()
    acc[...] = jnp.zeros_like(acc)
    own.wait()

    def block(dy, dx, j):
        return x_all.at[row_of(dy, dx), spot(j)]

    def share(dy, dx, j):
        ref = block(dy, dx, j)
        send(ref, ref, p_s.at[dy, dx, j], p_r.at[dy, dx, j], partner)

    def z_event(j):
        ref = block(0, 0, j)
        arrive(ref, z_s.at[j], z_r.at[j])
        for d in far:
            send(ref, ref, x_s.at[d - 1, j], x_r.at[d - 1, j], x_dev(d))
            send(ref, ref, y_s.at[d - 1, j], y_r.at[d - 1, j], y_dev(d))
        share(0, 0, j)

    def xy_event(j):
        for d in far:
            ref = block(0, d, j)
            arrive(ref, x_s.at[d - 1, j], x_r.at[d - 1, j])
            top = ref.at[pl.ds(0, half)]
            for v in far:
                send(top, top, du_s.at[v - 1, d - 1, j], du_r.at[v - 1, d - 1, j], y_dev(v))
            share(0, d, j)
            ref = block(d, 0, j)
            arrive(ref, y_s.at[d - 1, j], y_r.at[d - 1, j])
            low = ref.at[pl.ds(half, half)]
            for v in far:
                send(low, low, dl_s.at[d - 1, v - 1, j], dl_r.at[d - 1, v - 1, j], x_dev(v))
            share(d, 0, j)

    def diag_event(j):
        for v in far:
            for d in far:
                ref = block(v, d, j)
                at = (v - 1, d - 1, j)
                arrive(ref.at[pl.ds(0, half)], du_s.at[at], du_r.at[at])
                arrive(ref.at[pl.ds(half, half)], dl_s.at[at], dl_r.at[at])
                share(v, d, j)

    def gate_event(j):
        ref = g_all.at[spot(j)]
        arrive(ref, gz_s.at[j], gz_r.at[j])
        send(ref, ref, gp_s.at[j], gp_r.at[j], partner)

    def ready(dy, dx):
        for j in levels:
            arrive(
                x_all.at[row_of(dy, dx), spot(j, 1 - core)], p_s.at[dy, dx, j], p_r.at[dy, dx, j]
            )

    def multiply(u):
        s, i = divmod(u, per)
        fetch(u).wait()
        left = x_all[row_of(*order[s])].reshape(2 * depth * rows, feat)
        acc[i] += jnp.dot(left, w_buf[u % slots], preferred_element_type=jnp.float32)
        if u + slots < units:
            fetch(u + slots).start()

    events = []
    for j in range(1, depth):
        events.append(functools.partial(z_event, j))
        events.append(functools.partial(xy_event, j - 1))
        if j >= 2:
            events.append(functools.partial(diag_event, j - 2))
    for event in events:
        event()
    for j in levels[1:]:
        gate_event(j)
    late = [functools.partial(xy_event, depth - 1)]
    late += [functools.partial(diag_event, j) for j in range(max(depth - 2, 0), depth)]
    stand = {per // 2: late[:1], 2 * per: late[1:2], 2 * per + per // 2: late[2:3]}
    ready(0, 0)
    for u in range(units):
        for event in stand.get(u, []):
            event()
        if u % per == 0 and u:
            ready(*order[u // per])
        multiply(u)

    for j in levels:
        arrive(g_all.at[spot(j, 1 - core)], gp_s.at[j], gp_r.at[j])

    def activate(b, _):
        at = pl.ds(pl.multiple_of(b * rows, rows), rows)
        for e in range(held):
            weight = jnp.sum(
                jnp.where(lane == col * held + e, g_all[b], 0.0), axis=1, keepdims=True
            )
            a, u = acc[2 * e, at, :], acc[2 * e + 1, at, :]
            value = a / (1.0 + jnp.exp(-a)) * u * weight
            hid[at, e * width : (e + 1) * width] = value.astype(jnp.bfloat16)
        return 0

    lax.fori_loop(0, 2 * depth, activate, 0)
    for down in downs:
        down.wait()

    def project(dy, dx, plane):
        rid = row_of(dy, dx)
        at = pl.ds(pl.multiple_of(plane * (depth * rows), rows), depth * rows)
        cols = pl.ds(pl.multiple_of(rid * feat, LANES), feat)
        value = jnp.dot(hid[at, :], wd[:, cols], preferred_element_type=jnp.float32)
        part[rid, pl.ds(plane * depth, depth)] = value.astype(jnp.bfloat16).reshape(
            depth, rows, feat
        )

    def swap(dy, dx):
        rid = row_of(dy, dx)
        send(
            part.at[rid, pl.ds((1 - core) * depth, depth)], pair.at[rid],
            q_s.at[dy, dx], q_r.at[dy, dx], partner,
        )

    def paired(dy, dx):
        arrive(pair.at[row_of(dy, dx)], q_s.at[dy, dx], q_r.at[dy, dx])

    def f32(value):
        return value.astype(jnp.float32)

    def both(dy, dx, j):
        rid = row_of(dy, dx)
        return f32(part[rid, spot(j)]) + f32(pair[rid, flip(zz, j)])

    back = [(v, d) for v in far for d in far]
    sides = [(0, d) for d in far] + [(d, 0) for d in far]
    falling = list(reversed(levels))

    def diag_out():
        for v, d in back:
            paired(v, d)
            for j in falling:
                ref = part.at[row_of(v, d), spot(j)]
                part[row_of(v, d), spot(j)] = both(v, d, j).astype(jnp.bfloat16)
                at = (v - 1, d - 1, j)
                send(ref.at[pl.ds(0, half)], dx_in.at[at], ou_s.at[at], ou_r.at[at], x_dev(d))
                send(ref.at[pl.ds(half, half)], dy_in.at[at], ol_s.at[at], ol_r.at[at], y_dev(v))

    todo = back + sides + [(0, 0)]
    for n, (dy, dx) in enumerate(todo):
        project(dy, dx, 1 - core)
        swap(dy, dx)
        if n == len(back):
            diag_out()
        project(dy, dx, core)

    for dy, dx in sides:
        paired(dy, dx)
    for j in falling:
        for d in far:
            total = both(0, d, j)
            top, low = total[:half], total[half:]
            for v in far:
                at = (v - 1, d - 1, j)
                arrive(dy_in.at[at], ol_s.at[at], ol_r.at[at])
                low = low + f32(dy_in[at])
            ref = part.at[row_of(0, d), spot(j)]
            ref[pl.ds(0, half), :] = top.astype(jnp.bfloat16)
            ref[pl.ds(half, half), :] = low.astype(jnp.bfloat16)
            send(ref, rx_in.at[d - 1, j], rx_s.at[d - 1, j], rx_r.at[d - 1, j], x_dev(d))
        for v in far:
            total = both(v, 0, j)
            top, low = total[:half], total[half:]
            for d in far:
                at = (v - 1, d - 1, j)
                arrive(dx_in.at[at], ou_s.at[at], ou_r.at[at])
                top = top + f32(dx_in[at])
            ref = part.at[row_of(v, 0), spot(j)]
            ref[pl.ds(0, half), :] = top.astype(jnp.bfloat16)
            ref[pl.ds(half, half), :] = low.astype(jnp.bfloat16)
            send(ref, ry_in.at[v - 1, j], ry_s.at[v - 1, j], ry_r.at[v - 1, j], y_dev(v))
    paired(0, 0)
    for j in falling:
        total = both(0, 0, j)
        for d in far:
            arrive(rx_in.at[d - 1, j], rx_s.at[d - 1, j], rx_r.at[d - 1, j])
            arrive(ry_in.at[d - 1, j], ry_s.at[d - 1, j], ry_r.at[d - 1, j])
            total = total + f32(rx_in[d - 1, j]) + f32(ry_in[d - 1, j])
        if j:
            ref = part.at[row, spot(j)]
            ref[...] = total.astype(jnp.bfloat16)
            send(ref, z_in.at[j - 1], oz_s.at[j], oz_r.at[j], z_dev(j))
    for j in falling[:-1]:
        arrive(z_in.at[j - 1], oz_s.at[j], oz_r.at[j])
        total = total + f32(z_in[j - 1])
    out[...] = total.astype(jnp.bfloat16)
    for copy in sent:
        copy.wait_send()


def one_kernel(tokens, routes, gates, w_gate, w_up, w_down):
    rows, feat = tokens.shape
    held, dim, width = w_gate.shape
    row_count, col_count = lax.axis_size("row"), lax.axis_size("col")
    side, depth = math.isqrt(row_count), col_count // 2
    f, half, bf, ff = side - 1, rows // 2, jnp.bfloat16, jnp.float32
    dma = pltpu.SemaphoreType.DMA
    slots = 4 * held
    vmem = pl.BlockSpec(memory_space=pltpu.VMEM)
    anywhere = pl.BlockSpec(memory_space=pl.ANY)
    return pl.pallas_call(
        functools.partial(kernel, side, depth),
        out_shape=jax.ShapeDtypeStruct((rows, feat), bf),
        in_specs=[vmem] * 3 + [anywhere] * 3,
        out_specs=vmem,
        scratch_shapes=[
            pltpu.VMEM((row_count, col_count, rows, feat), bf),
            pltpu.VMEM((col_count, rows, LANES), ff),
            pltpu.VMEM((slots, feat, width), bf),
            pltpu.VMEM((held * width, dim), bf),
            pltpu.VMEM((2 * held, col_count * rows, width), ff),
            pltpu.VMEM((col_count * rows, held * width), bf),
            pltpu.VMEM((row_count, col_count, rows, feat), bf),
            pltpu.VMEM((row_count, depth, rows, feat), bf),
            pltpu.VMEM((f, f, depth, half, feat), bf),
            pltpu.VMEM((f, f, depth, half, feat), bf),
            pltpu.VMEM((f, depth, rows, feat), bf),
            pltpu.VMEM((f, depth, rows, feat), bf),
            pltpu.VMEM((depth - 1, rows, feat), bf),
        ]
        + [dma((depth,))] * 6
        + [dma((f, depth))] * 4
        + [dma((f, f, depth))] * 4
        + [dma((side, side, depth))] * 2
        + [dma((slots,)), dma((held,)), dma]
        + [dma((side, side))] * 2
        + [dma((f, f, depth))] * 4
        + [dma((f, depth))] * 4
        + [dma((depth,))] * 2,
        compiler_params=pltpu.CompilerParams(
            collective_id=0, has_side_effects=True, vmem_limit_bytes=67043328
        ),
    )(tokens, routes, gates, w_gate, w_up, w_down)


def collectives(tokens, routes, gates, w_gate, w_up, w_down):
    held = w_gate.shape[0]
    expert_count = held * lax.axis_size("col")
    ids = jnp.arange(expert_count, dtype=jnp.int32)
    dense = jnp.sum(
        jnp.where(routes[:, :, None] == ids[None, None, :], gates[:, :, None], 0.0), axis=1
    )
    dense = lax.all_gather(dense, "col", axis=0, tiled=True)
    mine = lax.dynamic_slice_in_dim(dense, lax.axis_index("col") * held, held, axis=1)
    whole = lax.all_gather(tokens, "col", axis=0, tiled=True)
    whole = lax.all_gather(whole, "row", axis=1, tiled=True)
    gate_act = jnp.einsum("td,edf->etf", whole, w_gate, preferred_element_type=jnp.float32)
    up_act = jnp.einsum("td,edf->etf", whole, w_up, preferred_element_type=jnp.float32)
    hidden = jax.nn.silu(gate_act) * up_act * mine.T[:, :, None]
    total = jnp.einsum(
        "etf,efd->td", hidden.astype(jnp.bfloat16), w_down, preferred_element_type=jnp.float32
    ).astype(jnp.bfloat16)
    total = lax.psum_scatter(total, "row", scatter_dimension=1, tiled=True)
    return lax.psum_scatter(total, "col", scatter_dimension=0, tiled=True)


def shards(tokens, routes, gates, w_gate, w_up, w_down):
    row_count, col_count = lax.axis_size("row"), lax.axis_size("col")
    depth = col_count // 2
    fits = (
        tokens.shape[1] % LANES == 0
        and math.isqrt(row_count) ** 2 == row_count
        and row_count & (row_count - 1) == 0
        and depth >= 2
        and depth & (depth - 1) == 0
        and w_gate.shape[0] * col_count <= LANES
    )
    body = one_kernel if fits else collectives
    return body(tokens, routes, gates, w_gate, w_up, w_down)


def solution(mesh):
    return jax.shard_map(
        shards,
        mesh=mesh,
        in_specs=(
            P("col", "row"),
            P("col", None),
            P("col", None),
            P("col", None, "row"),
            P("col", None, "row"),
            P("col", "row", None),
        ),
        out_specs=P("col", "row"),
        check_vma=False,
    )
```

```python
import functools
import math

import jax
import jax.numpy as jnp
from jax import lax
from jax.experimental import pallas as pl
from jax.experimental.pallas import tpu as pltpu
from jax.sharding import PartitionSpec as P

MESH = pl.DeviceIdType.MESH
LANES = 128


def flip(value, mask):
    bit = 1
    while bit <= mask:
        if mask & bit:
            value = value + bit - 2 * bit * lax.rem(lax.div(value, bit), 2)
        bit *= 2
    return value


def kernel(
    side, depth, tokens, routes, gates, w_gate, w_up, w_down, out,
    x_all, g_all, w_buf, wd, acc, hid, part, pair, dx_in, dy_in, rx_in, ry_in, z_in,
    z_s, z_r, gz_s, gz_r, gp_s, gp_r, x_s, x_r, y_s, y_r, du_s, du_r, dl_s, dl_r,
    p_s, p_r, w_sem, wd_sem, own_sem,
    q_s, q_r, ou_s, ou_r, ol_s, ol_r, rx_s, rx_r, ry_s, ry_r, oz_s, oz_r,
):
    rows, feat = tokens.shape
    held, _, width = w_gate.shape
    half = rows // 2
    row, col = lax.axis_index("row"), lax.axis_index("col")
    yy, xx = lax.div(row, side), lax.rem(row, side)
    zz, core = lax.div(col, 2), lax.rem(col, 2)
    far = range(1, side)
    levels = range(depth)

    def row_of(dy, dx):
        return flip(yy, dy) * side + flip(xx, dx)

    def spot(j, plane=None):
        level = flip(zz, j)
        plane = core if plane is None else plane
        return lax.div(level, 2) * 4 + plane * 2 + lax.rem(level, 2)

    def band(p):
        return flip(lax.div(zz, 2), p)

    def band_rows(p):
        return pl.ds(pl.multiple_of(band(p) * (4 * rows), 4 * rows), 4 * rows)

    partner = (row, zz * 2 + 1 - core)

    def x_dev(dx):
        return (row_of(0, dx), col)

    def y_dev(dy):
        return (row_of(dy, 0), col)

    def z_dev(j):
        return (row, flip(zz, j) * 2 + core)

    sent = []

    def copy_of(src, dst, ss, rs, dev):
        return pltpu.make_async_remote_copy(
            src_ref=src, dst_ref=dst, send_sem=ss, recv_sem=rs,
            device_id=dev, device_id_type=MESH,
        )

    def send(src, dst, ss, rs, dev):
        copy = copy_of(src, dst, ss, rs, dev)
        copy.start()
        sent.append(copy)

    def arrive(ref, ss, rs):
        copy_of(ref, ref, ss, rs, partner).wait_recv()

    back = [(v, d) for v in far for d in far]
    sides = [(0, d) for d in far] + [(d, 0) for d in far]
    order = [(0, 0)] + sides + back
    bands = depth // 2
    per = 2 * held
    slots = w_buf.shape[0]
    units = bands * len(order) * per

    def fetch(u):
        s, i = divmod(u, per)
        e, m = divmod(i, 2)
        start = pl.multiple_of(row_of(*order[s % len(order)]) * feat, LANES)
        return pltpu.make_async_copy(
            (w_up if m else w_gate).at[e, pl.ds(start, feat), :],
            w_buf.at[u % slots],
            w_sem.at[u % slots],
        )

    for u in range(min(slots, units)):
        fetch(u).start()
    own = pltpu.make_async_copy(tokens, x_all.at[row, spot(0)], own_sem)
    own.start()

    lane = lax.broadcasted_iota(jnp.int32, (rows, LANES), 1)
    line = lax.broadcasted_iota(jnp.int32, (LANES, rows), 0)
    dense = jnp.zeros((LANES, rows), jnp.float32)
    for k in range(routes.shape[0]):
        dense = dense + jnp.where(line == routes[k : k + 1, :], gates[k : k + 1, :], 0.0)
    g_all[spot(0)] = dense.T

    barrier = pltpu.get_barrier_semaphore()
    peers = [partner] + [x_dev(d) for d in far] + [y_dev(d) for d in far]
    peers += [z_dev(j) for j in levels[1:]]
    for peer in peers:
        pl.semaphore_signal(barrier, inc=1, device_id=peer, device_id_type=MESH)
    pl.semaphore_wait(barrier, len(peers))

    mine = x_all.at[row, spot(0)]
    for d in far:
        send(tokens, mine, x_s.at[d - 1, 0], x_r.at[d - 1, 0], x_dev(d))
        send(tokens, mine, y_s.at[d - 1, 0], y_r.at[d - 1, 0], y_dev(d))
    send(tokens, mine, p_s.at[0, 0, 0], p_r.at[0, 0, 0], partner)
    own_gates = g_all.at[spot(0)]
    for j in levels[1:]:
        send(tokens, mine, z_s.at[j], z_r.at[j], z_dev(j))
        send(own_gates, own_gates, gz_s.at[j], gz_r.at[j], z_dev(j))
    send(own_gates, own_gates, gp_s.at[0], gp_r.at[0], partner)
    downs = [
        pltpu.make_async_copy(w_down.at[e], wd.at[pl.ds(e * width, width), :], wd_sem.at[e])
        for e in range(held)
    ]
    for down in downs:
        down.start()
    own.wait()

    def block(dy, dx, j):
        return x_all.at[row_of(dy, dx), spot(j)]

    def share(dy, dx, j):
        ref = block(dy, dx, j)
        send(ref, ref, p_s.at[dy, dx, j], p_r.at[dy, dx, j], partner)

    def z_event(j):
        ref = block(0, 0, j)
        arrive(ref, z_s.at[j], z_r.at[j])
        for d in far:
            send(ref, ref, x_s.at[d - 1, j], x_r.at[d - 1, j], x_dev(d))
            send(ref, ref, y_s.at[d - 1, j], y_r.at[d - 1, j], y_dev(d))
        share(0, 0, j)
        ref = g_all.at[spot(j)]
        arrive(ref, gz_s.at[j], gz_r.at[j])
        send(ref, ref, gp_s.at[j], gp_r.at[j], partner)

    def xy_event(j):
        for d in far:
            ref = block(0, d, j)
            arrive(ref, x_s.at[d - 1, j], x_r.at[d - 1, j])
            top = ref.at[pl.ds(0, half)]
            for v in far:
                send(top, top, du_s.at[v - 1, d - 1, j], du_r.at[v - 1, d - 1, j], y_dev(v))
            share(0, d, j)
            ref = block(d, 0, j)
            arrive(ref, y_s.at[d - 1, j], y_r.at[d - 1, j])
            low = ref.at[pl.ds(half, half)]
            for v in far:
                send(low, low, dl_s.at[d - 1, v - 1, j], dl_r.at[d - 1, v - 1, j], x_dev(v))
            share(d, 0, j)

    def diag_event(j):
        for v in far:
            for d in far:
                ref = block(v, d, j)
                at = (v - 1, d - 1, j)
                arrive(ref.at[pl.ds(0, half)], du_s.at[at], du_r.at[at])
                arrive(ref.at[pl.ds(half, half)], dl_s.at[at], dl_r.at[at])
                share(v, d, j)

    def multiply(p, s):
        dy, dx = order[s]
        for j in (2 * p, 2 * p + 1):
            arrive(
                x_all.at[row_of(dy, dx), spot(j, 1 - core)], p_s.at[dy, dx, j], p_r.at[dy, dx, j]
            )
        for i in range(per):
            u = (p * len(order) + s) * per + i
            fetch(u).wait()
            left = x_all[row_of(dy, dx), pl.ds(band(p) * 4, 4)].reshape(4 * rows, feat)
            value = jnp.dot(left, w_buf[u % slots], preferred_element_type=jnp.float32)
            if s:
                acc[i, band_rows(p), :] += value
            else:
                acc[i, band_rows(p), :] = value
            if u + slots < units:
                fetch(u + slots).start()

    def activate(p):
        for j in (2 * p, 2 * p + 1):
            arrive(g_all.at[spot(j, 1 - core)], gp_s.at[j], gp_r.at[j])

        def step(n, _):
            b = band(p) * 4 + n
            at = pl.ds(pl.multiple_of(b * rows, rows), rows)
            for e in range(held):
                weight = jnp.sum(
                    jnp.where(lane == col * held + e, g_all[b], 0.0), axis=1, keepdims=True
                )
                a, u = acc[2 * e, at, :], acc[2 * e + 1, at, :]
                value = a / (1.0 + jnp.exp(-a)) * u * weight
                hid[at, e * width : (e + 1) * width] = value.astype(jnp.bfloat16)
            return 0

        lax.fori_loop(0, 4, step, 0)
        if p == 0:
            for down in downs:
                down.wait()

    def swapped(dy, dx, p):
        return pair.at[row_of(dy, dx), pl.ds(band(p) * 2, 2)]

    def project(dy, dx, p):
        rid = row_of(dy, dx)
        cols = pl.ds(pl.multiple_of(rid * feat, LANES), feat)
        value = jnp.dot(hid[band_rows(p), :], wd[:, cols], preferred_element_type=jnp.float32)
        part[rid, pl.ds(band(p) * 4, 4)] = value.astype(jnp.bfloat16).reshape(4, rows, feat)
        send(
            part.at[rid, pl.ds(band(p) * 4 + (1 - core) * 2, 2)], swapped(dy, dx, p),
            q_s.at[dy, dx, p], q_r.at[dy, dx, p], partner,
        )

    def paired(dy, dx, p):
        arrive(swapped(dy, dx, p), q_s.at[dy, dx, p], q_r.at[dy, dx, p])

    def f32(value):
        return value.astype(jnp.float32)

    def both(dy, dx, j):
        rid = row_of(dy, dx)
        return f32(part[rid, spot(j)]) + f32(pair[rid, flip(zz, j)])

    falling = list(reversed(levels))

    def diag_out(p):
        for v, d in back:
            paired(v, d, p)
            for j in (2 * p + 1, 2 * p):
                ref = part.at[row_of(v, d), spot(j)]
                part[row_of(v, d), spot(j)] = both(v, d, j).astype(jnp.bfloat16)
                at = (v - 1, d - 1, j)
                send(ref.at[pl.ds(0, half)], dx_in.at[at], ou_s.at[at], ou_r.at[at], x_dev(d))
                send(ref.at[pl.ds(half, half)], dy_in.at[at], ol_s.at[at], ol_r.at[at], y_dev(v))

    near = 1 + len(sides)
    z_event(1)
    for p in range(bands):
        more = p + 1 < bands
        multiply(p, 0)
        if p == 0:
            xy_event(0)
        xy_event(2 * p + 1)
        for s in range(1, near):
            multiply(p, s)
            if more and s == 1:
                z_event(2 * p + 2)
        diag_event(2 * p)
        if p:
            diag_out(p - 1)
        diag_event(2 * p + 1)
        for s in range(near, len(order)):
            multiply(p, s)
        if more:
            z_event(2 * p + 3)
        activate(p)
        for dy, dx in back:
            project(dy, dx, p)
        if more:
            xy_event(2 * p + 2)
        for n, (dy, dx) in enumerate(sides + [(0, 0)]):
            project(dy, dx, p)
            if not more and n == 0:
                diag_out(p)

    for j in falling:
        if j % 2:
            for dy, dx in sides:
                paired(dy, dx, j // 2)
        for d in far:
            total = both(0, d, j)
            top, low = total[:half], total[half:]
            for v in far:
                at = (v - 1, d - 1, j)
                arrive(dy_in.at[at], ol_s.at[at], ol_r.at[at])
                low = low + f32(dy_in[at])
            ref = part.at[row_of(0, d), spot(j)]
            ref[pl.ds(0, half), :] = top.astype(jnp.bfloat16)
            ref[pl.ds(half, half), :] = low.astype(jnp.bfloat16)
            send(ref, rx_in.at[d - 1, j], rx_s.at[d - 1, j], rx_r.at[d - 1, j], x_dev(d))
        for v in far:
            total = both(v, 0, j)
            top, low = total[:half], total[half:]
            for d in far:
                at = (v - 1, d - 1, j)
                arrive(dx_in.at[at], ou_s.at[at], ou_r.at[at])
                top = top + f32(dx_in[at])
            ref = part.at[row_of(v, 0), spot(j)]
            ref[pl.ds(0, half), :] = top.astype(jnp.bfloat16)
            ref[pl.ds(half, half), :] = low.astype(jnp.bfloat16)
            send(ref, ry_in.at[v - 1, j], ry_s.at[v - 1, j], ry_r.at[v - 1, j], y_dev(v))
    for j in falling:
        if j % 2:
            paired(0, 0, j // 2)
        total = both(0, 0, j)
        for d in far:
            arrive(rx_in.at[d - 1, j], rx_s.at[d - 1, j], rx_r.at[d - 1, j])
            arrive(ry_in.at[d - 1, j], ry_s.at[d - 1, j], ry_r.at[d - 1, j])
            total = total + f32(rx_in[d - 1, j]) + f32(ry_in[d - 1, j])
        if j:
            ref = part.at[row, spot(j)]
            ref[...] = total.astype(jnp.bfloat16)
            send(ref, z_in.at[j - 1], oz_s.at[j], oz_r.at[j], z_dev(j))
    for j in falling[:-1]:
        arrive(z_in.at[j - 1], oz_s.at[j], oz_r.at[j])
        total = total + f32(z_in[j - 1])
    out[...] = total.astype(jnp.bfloat16)
    for copy in sent:
        copy.wait_send()


def one_kernel(tokens, routes, gates, w_gate, w_up, w_down):
    rows, feat = tokens.shape
    held, dim, width = w_gate.shape
    row_count, col_count = lax.axis_size("row"), lax.axis_size("col")
    side, depth = math.isqrt(row_count), col_count // 2
    f, half, bf, ff = side - 1, rows // 2, jnp.bfloat16, jnp.float32
    dma = pltpu.SemaphoreType.DMA
    slots = 4 * held
    vmem = pl.BlockSpec(memory_space=pltpu.VMEM)
    anywhere = pl.BlockSpec(memory_space=pl.ANY)
    return pl.pallas_call(
        functools.partial(kernel, side, depth),
        out_shape=jax.ShapeDtypeStruct((rows, feat), bf),
        in_specs=[vmem] * 3 + [anywhere] * 3,
        out_specs=vmem,
        scratch_shapes=[
            pltpu.VMEM((row_count, col_count, rows, feat), bf),
            pltpu.VMEM((col_count, rows, LANES), ff),
            pltpu.VMEM((slots, feat, width), bf),
            pltpu.VMEM((held * width, dim), bf),
            pltpu.VMEM((2 * held, col_count * rows, width), ff),
            pltpu.VMEM((col_count * rows, held * width), bf),
            pltpu.VMEM((row_count, col_count, rows, feat), bf),
            pltpu.VMEM((row_count, depth, rows, feat), bf),
            pltpu.VMEM((f, f, depth, half, feat), bf),
            pltpu.VMEM((f, f, depth, half, feat), bf),
            pltpu.VMEM((f, depth, rows, feat), bf),
            pltpu.VMEM((f, depth, rows, feat), bf),
            pltpu.VMEM((depth - 1, rows, feat), bf),
        ]
        + [dma((depth,))] * 6
        + [dma((f, depth))] * 4
        + [dma((f, f, depth))] * 4
        + [dma((side, side, depth))] * 2
        + [dma((slots,)), dma((held,)), dma]
        + [dma((side, side, depth // 2))] * 2
        + [dma((f, f, depth))] * 4
        + [dma((f, depth))] * 4
        + [dma((depth,))] * 2,
        compiler_params=pltpu.CompilerParams(
            collective_id=0, has_side_effects=True, vmem_limit_bytes=67043328
        ),
    )(tokens, routes.T, gates.T, w_gate, w_up, w_down)


def collectives(tokens, routes, gates, w_gate, w_up, w_down):
    held = w_gate.shape[0]
    expert_count = held * lax.axis_size("col")
    ids = jnp.arange(expert_count, dtype=jnp.int32)
    dense = jnp.sum(
        jnp.where(routes[:, :, None] == ids[None, None, :], gates[:, :, None], 0.0), axis=1
    )
    dense = lax.all_gather(dense, "col", axis=0, tiled=True)
    mine = lax.dynamic_slice_in_dim(dense, lax.axis_index("col") * held, held, axis=1)
    whole = lax.all_gather(tokens, "col", axis=0, tiled=True)
    whole = lax.all_gather(whole, "row", axis=1, tiled=True)
    gate_act = jnp.einsum("td,edf->etf", whole, w_gate, preferred_element_type=jnp.float32)
    up_act = jnp.einsum("td,edf->etf", whole, w_up, preferred_element_type=jnp.float32)
    hidden = jax.nn.silu(gate_act) * up_act * mine.T[:, :, None]
    total = jnp.einsum(
        "etf,efd->td", hidden.astype(jnp.bfloat16), w_down, preferred_element_type=jnp.float32
    ).astype(jnp.bfloat16)
    total = lax.psum_scatter(total, "row", scatter_dimension=1, tiled=True)
    return lax.psum_scatter(total, "col", scatter_dimension=0, tiled=True)


def shards(tokens, routes, gates, w_gate, w_up, w_down):
    row_count, col_count = lax.axis_size("row"), lax.axis_size("col")
    depth = col_count // 2
    fits = (
        tokens.shape[1] % LANES == 0
        and math.isqrt(row_count) ** 2 == row_count
        and row_count & (row_count - 1) == 0
        and depth >= 2
        and depth & (depth - 1) == 0
        and w_gate.shape[0] * col_count <= LANES
    )
    body = one_kernel if fits else collectives
    return body(tokens, routes, gates, w_gate, w_up, w_down)


def solution(mesh):
    return jax.shard_map(
        shards,
        mesh=mesh,
        in_specs=(
            P("col", "row"),
            P("col", None),
            P("col", None),
            P("col", None, "row"),
            P("col", None, "row"),
            P("col", "row", None),
        ),
        out_specs=P("col", "row"),
        check_vma=False,
    )
```
